32 devices in a mesh: sub: 8 (over z, y), band: 4 (over x, core).
Axes of the slice: x: 2, y: 2, z: 4, core: 2. Of those that a mesh axis runs over, the one named last changes fastest.
Arguments:
- intensity: bfloat16 [4, 4096, 8192], P(None, ('band', 'sub')), may hold values from -6 to 6
- channel_spans: int32 [4096], replicated, may hold values from 1 to 8
Outputs:
- dedispersed: float32 [4, 512, 8192], P(None, ('band', 'sub'))
- peak_snr: float32 [4, 512, 8192], P(None, ('band', 'sub'))
The draws below stay inside these ranges and needn't reach their ends.
All inputs are finite; a program needn't handle non-finite values.
Results may differ from the reference program's by a relative error of at most 0.0003.
Values sent between devices are 32-bit elements; how exact they have to be, the bound alone decides.
No kernel may reach another device: no remote copies, remote signals or barrier semaphores. Data moves between devices by JAX's collectives and lax.ppermute only.
A program may use at most 128 MiB of HBM per device.

```python
import math
import jax
import jax.numpy as jnp
import numpy as np
from jax import lax

CHAN_DEV = 128
ROWS_DEV = 16
BEAMS = 4
SAMPLES = 8192
BOXES = 9
CH = 4096
DM = 512
DEVICES = 32


def plant(values, rng, smallest, high):
    longest = values.shape.index(max(values.shape))
    spots = []
    for shift in (0, 1):
        where = [jax.random.randint(jax.random.fold_in(rng, axis), (), 0, length) for axis, length in enumerate(values.shape)]
        where[longest] = (where[longest] + shift) % values.shape[longest]
        spots.append(tuple(where))
    return values.at[spots[0]].set(smallest).at[spots[1]].set(high)


def block_scale(key, shape, cuts, smallest, largest):
    loudness, own = 1.0, jax.random.fold_in(key, 6)
    for axis_at, parts in cuts:
        heights = jnp.exp(jax.random.uniform(jax.random.fold_in(own, axis_at), (parts,), jnp.float32, smallest / len(cuts), largest / len(cuts)))
        loudness = loudness * jnp.repeat(heights, shape[axis_at] // parts).reshape([-1 if axis == axis_at else 1 for axis in range(len(shape))])
    return loudness


def bell_draw(key, shape, deviation, limit, cuts=(), kind=jnp.bfloat16):
    values = deviation * jax.random.normal(key, shape, jnp.float32)
    if cuts:
        values = values * block_scale(key, shape, cuts, -0.22, 0.18)
    return jnp.clip(values, -limit, limit).astype(kind)


def setup_inputs(seed: int = 0) -> dict:
    seeds = jax.random.split(jax.random.key(seed), 3)
    return {
        "intensity": bell_draw(seeds[0], (BEAMS, CH, SAMPLES), 1.0, 6.0, ((1, 32),)),
        "channel_spans": plant(jax.random.randint(seeds[1], (CH,), 1, 9), jax.random.fold_in(seeds[1], 1), 1, 8).astype(jnp.int32),
    }


def reverse_bits(value, bit_total):
    result = 0
    for position in range(bit_total):
        result = result | (value >> position & 1) << bit_total - 1 - position
    return result

def shift_rows(row_data, shifts, margin):
    length = row_data.shape[1]
    padded = jnp.pad(row_data, ((0, 0), (margin, 0)))
    return jax.vmap(lambda one_row, one_shift: lax.dynamic_slice_in_dim(one_row, margin - one_shift, length))(padded, shifts)

def dedisperse_beam(one_beam, channel_spans):
    delay_plane = one_beam.astype(jnp.float32)[:, None, :]
    level_total = CH.bit_length() - 1
    previous_rows = 1
    for tree_level in range(1, level_total + 1):
        row_count = max(1, 2 ** tree_level * ROWS_DEV // CHAN_DEV)
        band_count = CH >> tree_level
        lower_half = delay_plane[0::2]
        upper_half = delay_plane[1::2]
        if row_count > previous_rows:
            lower_half = jnp.repeat(lower_half, row_count // previous_rows, axis=1)
            upper_half = jnp.repeat(upper_half, row_count // previous_rows, axis=1)
        grouped = channel_spans.reshape(band_count, 2, 2 ** (tree_level - 1)).sum(axis=2).astype(jnp.int32)
        row_index = jnp.arange(row_count, dtype=jnp.int32)
        shifts = row_index[None, :] * grouped[:, 0:1] // (grouped[:, 0:1] + grouped[:, 1:2])
        shifted = shift_rows(upper_half.reshape(band_count * row_count, SAMPLES), shifts.reshape(-1), row_count)
        delay_plane = lower_half + shifted.reshape(band_count, row_count, SAMPLES)
        previous_rows = row_count
    top_plane = delay_plane[0]
    bit_total = DEVICES.bit_length() - 1
    reversal = np.array([reverse_bits(value, bit_total) for value in range(DEVICES)], dtype=np.int32)
    ordered = top_plane.reshape(DEVICES, ROWS_DEV, SAMPLES)[reversal].reshape(DM, SAMPLES)
    dedispersed = ordered * (1.0 / math.sqrt(CH))
    running = dedispersed
    peak_value = dedispersed
    box_width = 1
    for doubling in range(BOXES - 1):
        running = running + jnp.pad(running, ((0, 0), (box_width, 0)))[:, :SAMPLES]
        box_width = box_width * 2
        peak_value = jnp.maximum(peak_value, running * (1.0 / math.sqrt(box_width)))
    return (dedispersed, peak_value)

def reference(intensity, channel_spans):
    dedispersed, peak_snr = lax.map(lambda one_beam: dedisperse_beam(one_beam, channel_spans), intensity)
    return (dedispersed, peak_snr)
```

```python
import functools
import math

import jax
import jax.numpy as jnp
from jax import lax
from jax.experimental import pallas as pl
from jax.experimental.pallas import tpu as pltpu
from jax.sharding import PartitionSpec as P

ROWS_DEV = 16
BOXES = 9
LANES = 128
HALF = ROWS_DEV // 2


def padding(longest_shift):
    return -(-(longest_shift // LANES + 1) // 8) * 8


def delayed(source, lead, row, shift, pad, tiles):
    coarse = shift // LANES
    fine = shift - coarse * LANES
    here = source[lead, row, pl.ds(pad - coarse, tiles), :]
    before = source[lead, row, pl.ds(pad - coarse - 1, tiles), :]
    lane = lax.broadcasted_iota(jnp.int32, (tiles, LANES), 1)
    mixed = jnp.where(lane < LANES - fine, here, before)
    return pltpu.roll(mixed, fine, 1)


def bit_of(number, position):
    return lax.shift_right_logical(number, jnp.int32(position)) & 1


def local_kernel(chan_dev, tiles, pad, info, spans, sums, power, keep, send, wide, level_a, level_b):
    device = info[0]
    groups = HALF
    span = chan_dev // groups
    zero = jnp.zeros((pad, LANES), jnp.float32)
    for m in range(1, groups, 2):
        for r in range(HALF):
            level_a[m, r, 0:pad, :] = zero
            level_b[m, r, 0:pad, :] = zero
    step = 1024 if (tiles * LANES) % 1024 == 0 else LANES
    for start in range(0, tiles * LANES, step):
        part = jnp.dot(
            sums[...], power[0, :, start : start + step], preferred_element_type=jnp.float32
        )
        for piece in range(step // LANES):
            wide[start // LANES + piece] = part[:, piece * LANES : (piece + 1) * LANES]
    for m in range(groups):
        level_a[m, 0, pad : pad + tiles, :] = wide[:, m, :]
    widths = []
    for m in range(groups):
        total = spans[device * chan_dev + m * span]
        for c in range(1, span):
            total = total + spans[device * chan_dev + m * span + c]
        widths.append(total)
    source, target = level_a, level_b
    rows = 4
    bands = groups // 2
    old_rows = 1
    while True:
        last = rows == ROWS_DEV
        merged = []
        for m in range(bands):
            low, both = widths[2 * m], widths[2 * m] + widths[2 * m + 1]
            merged.append(both)
            if last:
                mine = bit_of(device, 0)
                for half, ref in ((mine, keep), (1 - mine, send)):

                    def body(i, carry, half=half, ref=ref, low=low, both=both, source=source):
                        r = half * HALF + i
                        shift = (r * low) // both
                        q = r // 2
                        ref[0, i] = source[0, q, pad : pad + tiles, :] + delayed(
                            source, 1, q, shift, pad, tiles
                        )
                        return carry

                    lax.fori_loop(0, HALF, body, 0)
            else:
                for r in range(rows):
                    q = r * old_rows // rows
                    shift = (r * low) // both
                    result = source[2 * m, q, pad : pad + tiles, :]
                    if r < 2:
                        result = result + source[2 * m + 1, q, pad : pad + tiles, :]
                    else:
                        result = result + delayed(source, 2 * m + 1, q, shift, pad, tiles)
                    target[m, r, pad : pad + tiles, :] = result
        if last:
            break
        widths = merged
        source, target = target, source
        old_rows, rows, bands = rows, rows * 2, bands // 2


def merge_rows(step, tiles, pad, info, kept, came, held, sems):
    device = info[0]
    mine = bit_of(device, step)
    copies = [
        pltpu.make_async_copy(kept.at[0], held.at[mine, :, pl.ds(pad, tiles), :], sems.at[0]),
        pltpu.make_async_copy(came.at[0], held.at[1 - mine, :, pl.ds(pad, tiles), :], sems.at[1]),
    ]
    for copy in copies:
        copy.start()
    zero = jnp.zeros((pad, LANES), jnp.float32)
    for q in range(HALF):
        held[1, q, 0:pad, :] = zero
    block = jnp.int32(0)
    for position in range(step + 1):
        block = 2 * block + bit_of(device, position)
    size = 2**step
    first = (device // (2 * size)) * (2 * size)
    low = info[1 + first + size] - info[1 + first]
    both = info[1 + first + 2 * size] - info[1 + first]
    for copy in copies:
        copy.wait()

    def row(i):
        shift = ((block * ROWS_DEV + i) * low) // both
        q = i // 2
        return held[0, q, pl.ds(pad, tiles), :] + delayed(held, 1, q, shift, pad, tiles)

    return row


def merge_kernel(step, tiles, pad, info, kept, came, keep, send, held, sems):
    row = merge_rows(step, tiles, pad, info, kept, came, held, sems)
    following = bit_of(info[0], step + 1)
    for half, ref in ((1 - following, send), (following, keep)):

        def body(i, carry, half=half, ref=ref):
            ref[0, i] = row(half * HALF + i)
            return carry

        lax.fori_loop(0, HALF, body, 0)


def final_kernel(step, tiles, pad, scale, *refs):
    info, kept, came = refs[:3]
    plane, peak, held, flat, tops, sems = refs[-6:]
    row = merge_rows(step, tiles, pad, info, kept, came, held, sems)
    lane = lax.broadcasted_iota(jnp.int32, (tiles, LANES), 1)
    first = lax.broadcasted_iota(jnp.int32, (tiles, LANES), 0) == 0

    def body(i, carry):
        running = row(i) * scale
        flat[i] = running
        best = running
        width = 1
        for _ in range(BOXES - 1):
            before = jnp.where(first, 0.0, pltpu.roll(running, 1, 0))
            if width < LANES:
                mixed = jnp.where(lane < LANES - width, running, before)
                running = running + pltpu.roll(mixed, width, 1)
            else:
                running = running + before
            width = width * 2
            best = jnp.maximum(best, running * (1.0 / math.sqrt(width)))
        tops[i] = best
        return carry

    lax.fori_loop(0, ROWS_DEV, body, 0)
    for h in range(0, ROWS_DEV, 8):

        def out(j, carry, h=h):
            columns = pl.ds(pl.multiple_of(j * LANES, LANES), LANES)
            plane[0, h : h + 8, columns] = flat[h : h + 8, j, :]
            peak[0, h : h + 8, columns] = tops[h : h + 8, j, :]
            return carry

        lax.fori_loop(0, tiles, out, 0)


SMEM = pl.BlockSpec(memory_space=pltpu.SMEM)
HBM = pl.BlockSpec(memory_space=pltpu.HBM)


def swapped(value, axis, distance):
    mask = 2**distance
    return lax.ppermute(value, axis, [(s, s ^ mask) for s in range(lax.axis_size(axis))])


def on_device(intensity, channel_spans):
    beams, chan_dev, samples = intensity.shape
    sub_count = lax.axis_size("sub")
    band_size = lax.axis_size("band")
    devices = sub_count * band_size
    tiles = samples // LANES
    sub_bits = sub_count.bit_length() - 1
    bits = devices.bit_length() - 1
    device = lax.axis_index("band") * sub_count + lax.axis_index("sub")
    totals = channel_spans.reshape(devices, chan_dev).sum(axis=1)
    edge = jnp.arange(devices + 1)[:, None] > jnp.arange(devices)[None, :]
    edges = jnp.where(edge, totals[None, :], 0).sum(axis=1)
    info = jnp.concatenate([device.reshape(1), edges]).astype(jnp.int32)
    place = device.reshape(1).astype(jnp.int32)
    group = jnp.arange(chan_dev) // (chan_dev // HALF)
    sums = (jnp.arange(HALF)[:, None] == group[None, :]).astype(jnp.bfloat16)
    halves = jax.ShapeDtypeStruct((1, HALF, tiles, LANES), jnp.float32)
    whole = jax.ShapeDtypeStruct((beams, ROWS_DEV, samples), jnp.float32)
    block = pl.BlockSpec((1, HALF, tiles, LANES), lambda i: (0, 0, 0, 0))
    size = HALF * tiles * LANES

    def local(beam):
        pad = padding(ROWS_DEV)
        return pl.pallas_call(
            functools.partial(local_kernel, chan_dev, tiles, pad),
            grid=(1,),
            in_specs=[
                SMEM,
                SMEM,
                pl.BlockSpec((HALF, chan_dev), lambda i: (0, 0)),
                pl.BlockSpec((1, chan_dev, samples), lambda i: (beam, 0, 0)),
            ],
            out_specs=[block, block],
            out_shape=[halves, halves],
            scratch_shapes=[
                pltpu.VMEM((tiles, HALF, LANES), jnp.float32),
                pltpu.VMEM((HALF, HALF, pad + tiles, LANES), jnp.float32),
                pltpu.VMEM((HALF, HALF, pad + tiles, LANES), jnp.float32),
            ],
            cost_estimate=pl.CostEstimate(
                flops=size * 40, bytes_accessed=chan_dev * samples * 2 + size * 8, transcendentals=0
            ),
            name="local",
        )(place, channel_spans, sums, intensity)

    def merge(step, kept, came):
        pad = padding(ROWS_DEV * 2 ** (step + 1))
        return pl.pallas_call(
            functools.partial(merge_kernel, step, tiles, pad),
            grid=(1,),
            in_specs=[SMEM, HBM, HBM],
            out_specs=[block, block],
            out_shape=[halves, halves],
            scratch_shapes=[
                pltpu.VMEM((2, HALF, pad + tiles, LANES), jnp.float32),
                pltpu.SemaphoreType.DMA((2,)),
            ],
            cost_estimate=pl.CostEstimate(
                flops=size * 8, bytes_accessed=size * 16, transcendentals=0
            ),
            name=f"merge{step}",
        )(info, kept, came)

    def final(beam, kept, came, done):
        step = bits - 1
        pad = padding(ROWS_DEV * 2**bits)
        rows = pl.BlockSpec((1, ROWS_DEV, samples), lambda i: (beam, 0, 0))
        return pl.pallas_call(
            functools.partial(
                final_kernel, step, tiles, pad, 1.0 / math.sqrt(chan_dev * devices)
            ),
            grid=(1,),
            in_specs=[SMEM, HBM, HBM] + [HBM] * len(done),
            out_specs=[rows, rows],
            out_shape=[whole, whole],
            scratch_shapes=[
                pltpu.VMEM((2, HALF, pad + tiles, LANES), jnp.float32),
                pltpu.VMEM((ROWS_DEV, tiles, LANES), jnp.float32),
                pltpu.VMEM((ROWS_DEV, tiles, LANES), jnp.float32),
                pltpu.SemaphoreType.DMA((2,)),
            ],
            input_output_aliases={3 + i: i for i in range(len(done))},
            cost_estimate=pl.CostEstimate(
                flops=size * 80, bytes_accessed=size * 24, transcendentals=0
            ),
            name="final",
        )(info, kept, came, *done)

    state = [local(beam) for beam in range(beams)]
    for step in range(bits):
        axis, distance = ("sub", step) if step < sub_bits else ("band", step - sub_bits)
        came = [swapped(send, axis, distance) for _, send in state]
        if step < bits - 1:
            state = [merge(step, state[b][0], came[b]) for b in range(beams)]
    done = ()
    for beam in range(beams):
        done = final(beam, state[beam][0], came[beam], done)
    return tuple(done)


def solution(mesh):
    spec = P(None, ("band", "sub"), None)
    return jax.shard_map(
        on_device, mesh=mesh, in_specs=(spec, P()), out_specs=(spec, spec), check_vma=False
    )
```

```python
import functools
import math

import jax
import jax.numpy as jnp
from jax import lax
from jax.experimental import pallas as pl
from jax.experimental.pallas import tpu as pltpu
from jax.sharding import PartitionSpec as P

ROWS_DEV = 16
BOXES = 9
LANES = 128
HALF = ROWS_DEV // 2


LANE_BITS = LANES.bit_length() - 1


def padding(longest_shift):
    return -(-(longest_shift // LANES + 1) // 8) * 8


def bit_of(number, position):
    return lax.shift_right_logical(number, jnp.int32(position)) & 1


def row_shifts(first_row, low, both, count):
    start = first_row * low
    shift = lax.div(start, both)
    rest = start - shift * both
    result = []
    for _ in range(count):
        result.append(shift)
        rest = rest + low
        over = rest >= both
        shift = jnp.where(over, shift + 1, shift)
        rest = jnp.where(over, rest - both, rest)
    return result


def delayed(source, lead, row, shift, pad, tiles):
    coarse = lax.shift_right_logical(shift, jnp.int32(LANE_BITS))
    fine = shift & (LANES - 1)
    here = source[lead, row, pl.ds(pad - coarse, tiles), :]
    before = source[lead, row, pl.ds(pad - coarse - 1, tiles), :]
    lane = lax.broadcasted_iota(jnp.int32, (tiles, LANES), 1)
    mixed = jnp.where(lane < LANES - fine, here, before)
    return pltpu.roll(mixed, fine, 1)


def local_kernel(beam, chan_dev, tiles, pad, parts, info, spans, sums, power, keep, send, *scratch):
    stage, wide, level_a, level_b, sems = scratch
    piece = tiles * LANES // parts
    copies = []
    for part in range(parts):
        columns = pl.ds(part * piece, piece)
        copies.append(
            pltpu.make_async_copy(
                power.at[beam, :, columns], stage.at[:, columns], sems.at[part]
            )
        )
        copies[-1].start()
    device = info[0]
    groups = HALF
    span = chan_dev // groups
    zero = jnp.zeros((pad, LANES), jnp.float32)
    for m in range(1, groups, 2):
        for r in range(1 if m > 1 else HALF):
            level_a[m, r, 0:pad, :] = zero
        for r in range(4):
            if m < 4:
                level_b[m, r, 0:pad, :] = zero
    widths = []
    for m in range(groups):
        total = spans[device * chan_dev + m * span]
        for c in range(1, span):
            total = total + spans[device * chan_dev + m * span + c]
        widths.append(total)
    for part in range(parts):
        copies[part].wait()
        value = jnp.dot(
            sums[...],
            stage[:, part * piece : (part + 1) * piece],
            preferred_element_type=jnp.float32,
        )
        for tile in range(piece // LANES):
            wide[part * (piece // LANES) + tile] = value[:, tile * LANES : (tile + 1) * LANES]
    for m in range(1, groups, 2):
        level_a[m, 0, pad : pad + tiles, :] = wide[:, m, :]
    source, target = level_a, level_b
    rows = 4
    bands = groups // 2
    old_rows = 1

    def low_row(m, q):
        if old_rows == 1:
            return wide[:, m, :]
        return source[m, q, pad : pad + tiles, :]

    while rows < ROWS_DEV:
        merged = []
        for m in range(bands):
            low, both = widths[2 * m], widths[2 * m] + widths[2 * m + 1]
            merged.append(both)
            shifts = row_shifts(jnp.int32(0), low, both, rows)
            for r in range(rows):
                q = r * old_rows // rows
                result = low_row(2 * m, q)
                if r < 2:
                    result = result + source[2 * m + 1, q, pad : pad + tiles, :]
                else:
                    result = result + delayed(source, 2 * m + 1, q, shifts[r], pad, tiles)
                target[m, r, pad : pad + tiles, :] = result
        widths = merged
        source, target = target, source
        old_rows, rows, bands = rows, rows * 2, bands // 2
    low, both = widths[0], widths[0] + widths[1]
    emit_halves(bit_of(device, 0), row_shifts(jnp.int32(0), low, both, ROWS_DEV), source, keep, send, pad, tiles)


def emit_halves(mine, shifts, held, keep, send, pad, tiles):
    for half, ref in ((1 - mine, send), (mine, keep)):
        for i in range(HALF):
            shift = jnp.where(half == 1, shifts[HALF + i], shifts[i])
            q = half * (HALF // 2) + i // 2
            ref[i] = held[0, q, pad : pad + tiles, :] + delayed(held, 1, q, shift, pad, tiles)


def fetch(step, tiles, pad, info, kept, came, held):
    device = info[0]
    mine = bit_of(device, step)
    zero = jnp.zeros((pad, LANES), jnp.float32)
    for q in range(HALF):
        held[1, q, 0:pad, :] = zero
    for q in range(HALF):
        held[mine, q, pad : pad + tiles, :] = kept[q]
        held[1 - mine, q, pad : pad + tiles, :] = came[q]
    block = jnp.int32(0)
    for position in range(step + 1):
        block = 2 * block + bit_of(device, position)
    size = 2**step
    first = lax.shift_right_logical(device, jnp.int32(step + 1)) * (2 * size)
    low = info[1 + first + size] - info[1 + first]
    both = info[1 + first + 2 * size] - info[1 + first]
    return row_shifts(block * ROWS_DEV, low, both, ROWS_DEV)


def merge_kernel(step, tiles, pad, info, kept, came, keep, send, held):
    shifts = fetch(step, tiles, pad, info, kept, came, held)
    emit_halves(bit_of(info[0], step + 1), shifts, held, keep, send, pad, tiles)


def final_kernel(beam, step, tiles, pad, scale, *refs):
    info, kept, came = refs[:3]
    plane, peak, held, run_a, run_b, best, out_plane, out_peak, sems = refs[-9:]
    shifts = fetch(step, tiles, pad, info, kept, came, held)
    lane = lax.broadcasted_iota(jnp.int32, (tiles, LANES), 1)
    zero = jnp.zeros((8, LANES), jnp.float32)
    copies = []
    for group in range(0, ROWS_DEV, 8):
        for i in range(8):
            r = group + i
            run_a[i, 0:8, :] = zero
            run_b[i, 0:8, :] = zero
            value = held[0, r // 2, pad : pad + tiles, :] + delayed(
                held, 1, r // 2, shifts[r], pad, tiles
            )
            value = value * scale
            run_a[i, 8 : 8 + tiles, :] = value
            best[i] = value
        for j in range(tiles):
            out_plane[group : group + 8, j * LANES : (j + 1) * LANES] = run_a[:, 8 + j, :]
        copies.append(
            pltpu.make_async_copy(
                out_plane.at[pl.ds(group, 8)], plane.at[beam, pl.ds(group, 8)], sems.at[0, group // 8]
            )
        )
        copies[-1].start()
        source, target = run_a, run_b
        width = 1
        for level in range(BOXES - 1):
            for i in range(8):
                here = source[i, 8 : 8 + tiles, :]
                before = source[i, 7 : 7 + tiles, :]
                if width < LANES:
                    moved = pltpu.roll(jnp.where(lane < LANES - width, here, before), width, 1)
                else:
                    moved = before
                value = here + moved
                target[i, 8 : 8 + tiles, :] = value
                best[i] = jnp.maximum(best[i], value * (1.0 / math.sqrt(2 * width)))
            source, target = target, source
            width = width * 2
        for j in range(tiles):
            out_peak[group : group + 8, j * LANES : (j + 1) * LANES] = best[:, j, :]
        copies.append(
            pltpu.make_async_copy(
                out_peak.at[pl.ds(group, 8)], peak.at[beam, pl.ds(group, 8)], sems.at[1, group // 8]
            )
        )
        copies[-1].start()
    for copy in copies:
        copy.wait()


SMEM = pl.BlockSpec(memory_space=pltpu.SMEM)
VMEM = pl.BlockSpec(memory_space=pltpu.VMEM)
HBM = pl.BlockSpec(memory_space=pltpu.HBM)


def swapped(value, axis, distance):
    mask = 2**distance
    return lax.ppermute(value, axis, [(s, s ^ mask) for s in range(lax.axis_size(axis))])


def on_device(intensity, channel_spans):
    beams, chan_dev, samples = intensity.shape
    sub_count = lax.axis_size("sub")
    band_size = lax.axis_size("band")
    devices = sub_count * band_size
    tiles = samples // LANES
    sub_bits = sub_count.bit_length() - 1
    bits = devices.bit_length() - 1
    device = lax.axis_index("band") * sub_count + lax.axis_index("sub")
    totals = channel_spans.reshape(devices, chan_dev).sum(axis=1)
    edge = jnp.arange(devices + 1)[:, None] > jnp.arange(devices)[None, :]
    edges = jnp.where(edge, totals[None, :], 0).sum(axis=1)
    info = jnp.concatenate([device.reshape(1), edges]).astype(jnp.int32)
    place = device.reshape(1).astype(jnp.int32)
    group = jnp.arange(chan_dev) // (chan_dev // HALF)
    sums = (jnp.arange(HALF)[:, None] == group[None, :]).astype(jnp.bfloat16)
    halves = jax.ShapeDtypeStruct((HALF, tiles, LANES), jnp.float32)
    whole = jax.ShapeDtypeStruct((beams, ROWS_DEV, samples), jnp.float32)
    size = HALF * tiles * LANES
    parts = 4

    def local(beam):
        pad = padding(ROWS_DEV)
        padded = pltpu.VMEM((HALF, HALF, pad + tiles, LANES), jnp.float32)
        return pl.pallas_call(
            functools.partial(local_kernel, beam, chan_dev, tiles, pad, parts),
            in_specs=[SMEM, SMEM, VMEM, HBM],
            out_specs=[VMEM, VMEM],
            out_shape=[halves, halves],
            scratch_shapes=[
                pltpu.VMEM((chan_dev, samples), jnp.bfloat16),
                pltpu.VMEM((tiles, HALF, LANES), jnp.float32),
                padded,
                padded,
                pltpu.SemaphoreType.DMA((parts,)),
            ],
            compiler_params=pltpu.CompilerParams(vmem_limit_bytes=12 << 20),
            cost_estimate=pl.CostEstimate(
                flops=size * 40, bytes_accessed=chan_dev * samples * 2 + size * 8, transcendentals=0
            ),
            name="local",
        )(place, channel_spans, sums, intensity)

    def merge(step, kept, came):
        pad = padding(ROWS_DEV * 2 ** (step + 1))
        return pl.pallas_call(
            functools.partial(merge_kernel, step, tiles, pad),
            in_specs=[SMEM, VMEM, VMEM],
            out_specs=[VMEM, VMEM],
            out_shape=[halves, halves],
            scratch_shapes=[pltpu.VMEM((2, HALF, pad + tiles, LANES), jnp.float32)],
            compiler_params=pltpu.CompilerParams(vmem_limit_bytes=4 << 20),
            cost_estimate=pl.CostEstimate(
                flops=size * 8, bytes_accessed=size * 16, transcendentals=0
            ),
            name=f"merge{step}",
        )(info, kept, came)

    def final(beam, kept, came, done):
        step = bits - 1
        pad = padding(ROWS_DEV * 2**bits)
        run = pltpu.VMEM((8, 8 + tiles, LANES), jnp.float32)
        rows = pltpu.VMEM((ROWS_DEV, samples), jnp.float32)
        return pl.pallas_call(
            functools.partial(
                final_kernel, beam, step, tiles, pad, 1.0 / math.sqrt(chan_dev * devices)
            ),
            in_specs=[SMEM, VMEM, VMEM] + [HBM] * len(done),
            out_specs=[HBM, HBM],
            out_shape=[whole, whole],
            scratch_shapes=[
                pltpu.VMEM((2, HALF, pad + tiles, LANES), jnp.float32),
                run,
                run,
                pltpu.VMEM((8, tiles, LANES), jnp.float32),
                rows,
                rows,
                pltpu.SemaphoreType.DMA((2, ROWS_DEV // 8)),
            ],
            input_output_aliases={3 + i: i for i in range(len(done))},
            compiler_params=pltpu.CompilerParams(vmem_limit_bytes=12 << 20),
            cost_estimate=pl.CostEstimate(
                flops=size * 80, bytes_accessed=size * 24, transcendentals=0
            ),
            name="final",
        )(info, kept, came, *done)

    state = [local(beam) for beam in range(beams)]
    for step in range(bits):
        axis, distance = ("sub", step) if step < sub_bits else ("band", step - sub_bits)
        came = [swapped(send, axis, distance) for _, send in state]
        if step < bits - 1:
            state = [merge(step, state[b][0], came[b]) for b in range(beams)]
    done = ()
    for beam in range(beams):
        done = final(beam, state[beam][0], came[beam], done)
    return tuple(done)


def solution(mesh):
    spec = P(None, ("band", "sub"), None)
    return jax.shard_map(
        on_device, mesh=mesh, in_specs=(spec, P()), out_specs=(spec, spec), check_vma=False
    )
```

```python
import functools
import math

import jax
import jax.numpy as jnp
from jax import lax
from jax.experimental import pallas as pl
from jax.experimental.pallas import tpu as pltpu
from jax.sharding import PartitionSpec as P

ROWS_DEV = 16
BOXES = 9
LANES = 128
HALF = ROWS_DEV // 2


LANE_BITS = LANES.bit_length() - 1


def padding(longest_shift):
    return -(-(longest_shift // LANES + 1) // 8) * 8


def bit_of(number, position):
    return lax.shift_right_logical(number, jnp.int32(position)) & 1


class Ratio:
    def __init__(self, low, both, top):
        self.both = both
        self.powers = [(jnp.int32(0), low)]
        for _ in range(top - 1):
            self.powers.append(self.add(self.powers[-1], self.powers[-1]))

    def add(self, one, two):
        rest = one[1] + two[1]
        over = rest >= self.both
        whole = one[0] + two[0]
        return jnp.where(over, whole + 1, whole), jnp.where(over, rest - self.both, rest)

    def scaled(self, power, factor):
        whole, rest = self.powers[power]
        return whole * factor, rest * factor


def delayed(source, row, shift, pad, tiles):
    coarse = lax.shift_right_logical(shift, jnp.int32(LANE_BITS))
    fine = shift & (LANES - 1)
    here = source[row, pl.ds(pad - coarse, tiles), :]
    before = source[row, pl.ds(pad - coarse - 1, tiles), :]
    lane = lax.broadcasted_iota(jnp.int32, (tiles, LANES), 1)
    mixed = jnp.where(lane < LANES - fine, here, before)
    return pltpu.roll(mixed, fine, 1)


class Plan:
    def __init__(self, bits, row_bits, order):
        self.bits, self.row_bits, self.order = bits, row_bits, order

    def free(self, merged, exchanged):
        return [p for p in range(self.row_bits + merged) if p not in exchanged]

    def stage(self, count):
        merged, open_bits = 0, []
        for position in range(count):
            open_bits = [self.order[position]] + open_bits
            if position < count - 1:
                while merged in open_bits:
                    open_bits = [p for p in open_bits if p != merged]
                    merged += 1
        return merged, open_bits


def row_tables(plan, info, merged, sources, exchanged):
    device = info[0]
    base = device
    for position, value in sources.items():
        base = (base & ~(1 << position)) | (value << position)
    size = 2**merged
    first = lax.shift_right_logical(base, jnp.int32(merged + 1)) * (2 * size)
    low = info[1 + first + size] - info[1 + first]
    both = info[1 + first + 2 * size] - info[1 + first]
    total = plan.row_bits + merged + 1
    ratio = Ratio(low, both, total)
    start = (jnp.int32(0), jnp.int32(0))
    for position in range(total):
        if position in exchanged:
            start = ratio.add(start, ratio.scaled(total - 1 - position, bit_of(device, position)))
    table = [start]
    for position in range(total):
        if position not in exchanged:
            power = ratio.powers[total - 1 - position]
            table = [value for old in table for value in (old, ratio.add(old, power))]
    return [value[0] for value in table]


def place(open_bits, sources):
    index = 0
    for position in open_bits:
        index = 2 * index + sources[position]
    return index


def combos(open_bits):
    result = [{}]
    for position in open_bits:
        result = [{**old, position: value} for old in result for value in (0, 1)]
    return result


def merge_all(plan, tiles, pad, info, merged, open_bits, exchanged, held, other):
    source, target = held, other
    while True:
        rows = 2 ** (plan.row_bits - len(open_bits))
        if merged not in open_bits:
            def plain(sources, index, shift=None, source=source, open_bits=open_bits, rows=rows):
                return source[place(open_bits, sources) * rows + index, pad : pad + tiles, :]

            return open_bits, merged, plain, None
        left = [p for p in open_bits if p != merged]
        tables = {}
        for number, sources in enumerate(combos(left)):
            tables[number] = row_tables(plan, info, merged, sources, exchanged)

        def row(sources, index, shift, source=source, open_bits=open_bits, rows=rows, merged=merged):
            low = place(open_bits, {**sources, merged: 0}) * rows
            high = place(open_bits, {**sources, merged: 1}) * rows
            half = lax.shift_right_logical(index, jnp.int32(1)) if hasattr(index, "dtype") else index // 2
            return source[low + half, pad : pad + tiles, :] + delayed(
                source, high + half, shift, pad, tiles
            )

        if merged + 1 not in left:
            return left, merged + 1, row, tables
        for number, sources in enumerate(combos(left)):
            for index in range(2 * rows):
                target[number * 2 * rows + index, pad : pad + tiles, :] = row(
                    sources, index, tables[number][index]
                )
        source, target = target, source
        open_bits, merged = left, merged + 1


def emit_halves(plan, info, merged, open_bits, exchanged, following, row, tables, keep, send):
    mine = bit_of(info[0], following)
    free = plan.free(merged, exchanged)
    weight = 2 ** (len(free) - 1 - free.index(following))
    count = 2 ** len(free)
    for number, sources in enumerate(combos(open_bits)):
        for half, ref in ((1 - mine, send), (mine, keep)):
            slot = 0
            for index in range(count):
                if index & weight:
                    continue
                shift = None
                if tables is not None:
                    shift = jnp.where(half == 1, tables[number][index + weight], tables[number][index])
                ref[number * (count // 2) + slot] = row(sources, index + half * weight, shift)
                slot += 1


def local_kernel(plan, beam, chan_dev, tiles, pad, parts, info, spans, sums, power, keep, send, *scratch):
    stage, wide, level_a, level_b, sems = scratch
    piece = tiles * LANES // parts
    copies = []
    for part in range(parts):
        columns = pl.ds(part * piece, piece)
        copies.append(
            pltpu.make_async_copy(
                power.at[beam, :, columns], stage.at[:, columns], sems.at[part]
            )
        )
        copies[-1].start()
    device = info[0]
    groups = HALF
    span = chan_dev // groups
    zero = jnp.zeros((pad, LANES), jnp.float32)
    for m in range(2 * HALF):
        level_a[m, 0:pad, :] = zero
        level_b[m, 0:pad, :] = zero
    widths = []
    for m in range(groups):
        total = spans[device * chan_dev + m * span]
        for c in range(1, span):
            total = total + spans[device * chan_dev + m * span + c]
        widths.append(total)
    for part in range(parts):
        copies[part].wait()
        value = jnp.dot(
            sums[...],
            stage[:, part * piece : (part + 1) * piece],
            preferred_element_type=jnp.float32,
        )
        for tile in range(piece // LANES):
            wide[part * (piece // LANES) + tile] = value[:, tile * LANES : (tile + 1) * LANES]
    for m in range(1, groups, 2):
        level_a[m, pad : pad + tiles, :] = wide[:, m, :]
    source, target = level_a, level_b
    rows = 4
    bands = groups // 2
    old_rows = 1

    def low_row(m, q):
        if old_rows == 1:
            return wide[:, m, :]
        return source[m * old_rows + q, pad : pad + tiles, :]

    def shifts_of(low, both):
        ratio = Ratio(low, both, max(1, (rows - 1).bit_length()))
        table = [(jnp.int32(0), jnp.int32(0))]
        for power in reversed(ratio.powers):
            table = [value for old in table for value in (old, ratio.add(old, power))]
        return [value[0] for value in table]

    while rows < ROWS_DEV:
        merged = []
        for m in range(bands):
            low, both = widths[2 * m], widths[2 * m] + widths[2 * m + 1]
            merged.append(both)
            shifts = shifts_of(low, both)
            for r in range(rows):
                q = r * old_rows // rows
                high = (2 * m + 1) * old_rows + q
                result = low_row(2 * m, q)
                if r < 2:
                    result = result + source[high, pad : pad + tiles, :]
                else:
                    result = result + delayed(source, high, shifts[r], pad, tiles)
                target[m * rows + r, pad : pad + tiles, :] = result
        widths = merged
        source, target = target, source
        old_rows, rows, bands = rows, rows * 2, bands // 2
    tables = {0: shifts_of(widths[0], widths[0] + widths[1])}

    def row(sources, index, shift):
        half = lax.shift_right_logical(index, jnp.int32(1))
        return source[half, pad : pad + tiles, :] + delayed(source, HALF + half, shift, pad, tiles)

    emit_halves(plan, info, 0, [], [], plan.order[0], row, tables, keep, send)


def fetch(plan, count, tiles, pad, info, kept, came, held, other):
    mine = bit_of(info[0], plan.order[count - 1])
    zero = jnp.zeros((pad, LANES), jnp.float32)
    for q in range(2 * HALF):
        held[q, 0:pad, :] = zero
        if other is not None:
            other[q, 0:pad, :] = zero
    for q in range(HALF):
        held[mine * HALF + q, pad : pad + tiles, :] = kept[q]
        held[(1 - mine) * HALF + q, pad : pad + tiles, :] = came[q]


def merge_kernel(plan, count, tiles, pad, info, kept, came, after, keep, send, held, other):
    del after
    merged, open_bits = plan.stage(count)
    exchanged = plan.order[:count]
    fetch(plan, count, tiles, pad, info, kept, came, held, other)
    open_bits, merged, row, tables = merge_all(
        plan, tiles, pad, info, merged, open_bits, exchanged, held, other
    )
    emit_halves(
        plan, info, merged, open_bits, exchanged, plan.order[count], row, tables, keep, send
    )


def final_kernel(plan, beam, tiles, pad, scale, *refs):
    info, kept, came = refs[:3]
    plane, peak, held, other, run_a, run_b, best, out_plane, out_peak, sems = refs[-10:]
    count = plan.bits
    merged, open_bits = plan.stage(count)
    fetch(plan, count, tiles, pad, info, kept, came, held, other)
    _, _, row, tables = merge_all(
        plan, tiles, pad, info, merged, open_bits, plan.order, held, other
    )
    lane = lax.broadcasted_iota(jnp.int32, (tiles, LANES), 1)
    zero = jnp.zeros((8, LANES), jnp.float32)
    copies = []
    for group in range(0, ROWS_DEV, 8):
        for i in range(8):
            run_a[i, 0:8, :] = zero
            run_b[i, 0:8, :] = zero
            value = row({}, group + i, tables[0][group + i]) * scale
            run_a[i, 8 : 8 + tiles, :] = value
            best[i] = value
        for j in range(tiles):
            out_plane[group : group + 8, j * LANES : (j + 1) * LANES] = run_a[:, 8 + j, :]
        copies.append(
            pltpu.make_async_copy(
                out_plane.at[pl.ds(group, 8)], plane.at[beam, pl.ds(group, 8)], sems.at[0, group // 8]
            )
        )
        copies[-1].start()
        source, target = run_a, run_b
        width = 1
        for level in range(BOXES - 1):
            for i in range(8):
                here = source[i, 8 : 8 + tiles, :]
                before = source[i, 7 : 7 + tiles, :]
                if width < LANES:
                    moved = pltpu.roll(jnp.where(lane < LANES - width, here, before), width, 1)
                else:
                    moved = before
                value = here + moved
                target[i, 8 : 8 + tiles, :] = value
                best[i] = jnp.maximum(best[i], value * (1.0 / math.sqrt(2 * width)))
            source, target = target, source
            width = width * 2
        for j in range(tiles):
            out_peak[group : group + 8, j * LANES : (j + 1) * LANES] = best[:, j, :]
        copies.append(
            pltpu.make_async_copy(
                out_peak.at[pl.ds(group, 8)], peak.at[beam, pl.ds(group, 8)], sems.at[1, group // 8]
            )
        )
        copies[-1].start()
    for copy in copies:
        copy.wait()


SMEM = pl.BlockSpec(memory_space=pltpu.SMEM)
VMEM = pl.BlockSpec(memory_space=pltpu.VMEM)
HBM = pl.BlockSpec(memory_space=pltpu.HBM)
ANY = pl.BlockSpec(memory_space=pl.ANY)


def swapped(value, axis, distance):
    mask = 2**distance
    return lax.ppermute(value, axis, [(s, s ^ mask) for s in range(lax.axis_size(axis))])


def allowed(wanted):
    left, order, merged = list(wanted), [], 0
    while left:
        bit = next(p for p in left if p < ROWS_DEV.bit_length() - 1 + merged)
        left.remove(bit)
        order.append(bit)
        while merged in order:
            merged += 1
    return order


def arrangement(bits, sub_bits, beams):
    far = sub_bits - 1
    near = list(range(far))
    rest = list(range(sub_bits, bits))
    kinds = [
        [far] + near + rest,
        near[:1] + [far] + near[1:] + rest,
        near + [far] + rest,
        near[:1] + rest[-1:] + near[1:] + rest[:-1] + [far],
    ]
    orders = [allowed(kinds[beam % len(kinds)]) for beam in range(beams)]
    schedule = [(beam, count) for count in range(bits + 1) for beam in range(beams)]
    return orders, schedule


def on_device(intensity, channel_spans):
    beams, chan_dev, samples = intensity.shape
    sub_count = lax.axis_size("sub")
    band_size = lax.axis_size("band")
    devices = sub_count * band_size
    tiles = samples // LANES
    sub_bits = sub_count.bit_length() - 1
    bits = devices.bit_length() - 1
    device = lax.axis_index("band") * sub_count + lax.axis_index("sub")
    totals = channel_spans.reshape(devices, chan_dev).sum(axis=1)
    edge = jnp.arange(devices + 1)[:, None] > jnp.arange(devices)[None, :]
    edges = jnp.where(edge, totals[None, :], 0).sum(axis=1)
    info = jnp.concatenate([device.reshape(1), edges]).astype(jnp.int32)
    spot = device.reshape(1).astype(jnp.int32)
    group = jnp.arange(chan_dev) // (chan_dev // HALF)
    sums = (jnp.arange(HALF)[:, None] == group[None, :]).astype(jnp.bfloat16)
    halves = jax.ShapeDtypeStruct((HALF, tiles, LANES), jnp.float32)
    whole = jax.ShapeDtypeStruct((beams, ROWS_DEV, samples), jnp.float32)
    size = HALF * tiles * LANES
    parts = 4

    row_bits = ROWS_DEV.bit_length() - 1
    orders, schedule = arrangement(bits, sub_bits, beams)
    plans = [Plan(bits, row_bits, order) for order in orders]
    pads = padding(ROWS_DEV * 2**bits)

    def local(beam, after):
        del after
        pad = padding(ROWS_DEV)
        padded = pltpu.VMEM((2 * HALF, pad + tiles, LANES), jnp.float32)
        return pl.pallas_call(
            functools.partial(local_kernel, plans[beam], beam, chan_dev, tiles, pad, parts),
            in_specs=[SMEM, SMEM, VMEM, HBM],
            out_specs=[VMEM, VMEM],
            out_shape=[halves, halves],
            scratch_shapes=[
                pltpu.VMEM((chan_dev, samples), jnp.bfloat16),
                pltpu.VMEM((tiles, HALF, LANES), jnp.float32),
                padded,
                padded,
                pltpu.SemaphoreType.DMA((parts,)),
            ],
            compiler_params=pltpu.CompilerParams(vmem_limit_bytes=12 << 20),
            cost_estimate=pl.CostEstimate(
                flops=size * 40, bytes_accessed=chan_dev * samples * 2 + size * 8, transcendentals=0
            ),
            name="local",
        )(spot, channel_spans, sums, intensity)

    def merge(beam, count, kept, came, after):
        padded = pltpu.VMEM((2 * HALF, pads + tiles, LANES), jnp.float32)
        return pl.pallas_call(
            functools.partial(merge_kernel, plans[beam], count, tiles, pads),
            in_specs=[SMEM, VMEM, VMEM, ANY],
            out_specs=[VMEM, VMEM],
            out_shape=[halves, halves],
            scratch_shapes=[padded, padded],
            compiler_params=pltpu.CompilerParams(vmem_limit_bytes=4 << 20),
            cost_estimate=pl.CostEstimate(
                flops=size * 8, bytes_accessed=size * 16, transcendentals=0
            ),
            name=f"merge{count}_{beam}",
        )(info, kept, came, after)

    def final(beam, kept, came, after, done):
        run = pltpu.VMEM((8, 8 + tiles, LANES), jnp.float32)
        rows = pltpu.VMEM((ROWS_DEV, samples), jnp.float32)
        padded = pltpu.VMEM((2 * HALF, pads + tiles, LANES), jnp.float32)
        extra = [after] if not done else []
        return pl.pallas_call(
            functools.partial(
                final_kernel, plans[beam], beam, tiles, pads, 1.0 / math.sqrt(chan_dev * devices)
            ),
            in_specs=[SMEM, VMEM, VMEM] + [ANY] * len(extra) + [HBM] * len(done),
            out_specs=[HBM, HBM],
            out_shape=[whole, whole],
            scratch_shapes=[
                padded,
                padded,
                run,
                run,
                pltpu.VMEM((8, tiles, LANES), jnp.float32),
                rows,
                rows,
                pltpu.SemaphoreType.DMA((2, ROWS_DEV // 8)),
            ],
            input_output_aliases={3 + i: i for i in range(len(done))},
            compiler_params=pltpu.CompilerParams(vmem_limit_bytes=12 << 20),
            cost_estimate=pl.CostEstimate(
                flops=size * 80, bytes_accessed=size * 24, transcendentals=0
            ),
            name=f"final_{beam}",
        )(info, kept, came, *extra, *done)

    done, after = (), None
    state, came = {}, {}
    for beam, count in schedule:
        if count == 0:
            kept, send = local(beam, after)
        elif count < bits:
            kept, send = merge(beam, count, state[beam], came[beam], after)
        else:
            done = final(beam, state[beam], came[beam], after, done)
            continue
        after = kept
        state[beam] = kept
        bit = orders[beam][count]
        axis, distance = ("sub", bit) if bit < sub_bits else ("band", bit - sub_bits)
        came[beam] = swapped(send, axis, distance)
    return tuple(done)


def solution(mesh):
    spec = P(None, ("band", "sub"), None)
    return jax.shard_map(
        on_device, mesh=mesh, in_specs=(spec, P()), out_specs=(spec, spec), check_vma=False
    )
```
